1024 devices in a mesh: band: 32 (over z_lo, y, core), col: 32 (over z_hi, x).
Axes of the slice: x: 8, y: 8, z: 8 (z_hi: 4, z_lo: 2; z = z_hi * 2 + z_lo), core: 2. Of those that a mesh axis runs over, the one named last changes fastest.
Arguments:
- intersections: bfloat16 [64, 4096, 512], P('band'), may hold values from -6 to 6
- screened: bfloat16 [4096, 4096], P('band', 'col'), may hold values from -0.09375 to 0.09375
- poles: bfloat16 [4096, 4096], P('band', 'col'), may hold values from 0.5 to 4
- gap_energy: float32 [3], replicated, may hold values from 0.3 to 3
- gap_class: int32 [64, 512], P('band'), may hold values from 0 to 2
Outputs:
- sigma: float32 [512, 512], P('band', 'col')
The draws below stay inside these ranges and needn't reach their ends.
All inputs are finite; a program needn't handle non-finite values.
Results may differ from the reference program's by a relative error of at most 0.0041.
Values may be sent and summed in bfloat16 or wider, within the bound.
No kernel may reach another device: no remote copies, remote signals or barrier semaphores. Data moves between devices by JAX's collectives and lax.ppermute only.
A program may use at most 64 MiB of HBM per device.

```python
import math
import jax
import jax.numpy as jnp
from jax import lax

S = 512
CLASSES = 3
NG = 4096
NB = 64


def touch_ends(entries, rng, least, high):
    dims = entries.shape
    place = [jax.random.randint(jax.random.fold_in(rng, axis), (), 0, dims[axis]) for axis in range(len(dims))]
    entries = entries.at[tuple(place)].set(least)
    longest = dims.index(max(dims))
    place[longest] = (place[longest] + 1) % dims[longest]
    return entries.at[tuple(place)].set(high)


def block_scale(own_key, extent, split, smallest, high):
    loudness = 1.0
    for dim, shards_of in split:
        steps = jax.random.uniform(jax.random.fold_in(jax.random.fold_in(own_key, 6), dim), (shards_of,), jnp.float32, smallest / len(split), high / len(split))
        loudness = loudness * jnp.repeat(jnp.exp(steps), extent[dim] // shards_of).reshape((-1,) + (1,) * (len(extent) - 1 - dim))
    return loudness


def scatter_about(key, dims, deviation, limit, shards=(), kind=jnp.bfloat16):
    array = deviation * jax.random.normal(key, dims, jnp.float32)
    if shards:
        array = array * block_scale(key, dims, shards, -0.22, 0.18)
    return jnp.clip(array, -limit, limit).astype(kind)


def setup_inputs(seed: int = 0) -> dict:
    key_of = jax.random.split(jax.random.key(seed), 6)
    intersections = scatter_about(key_of[0], (NB, NG, S), 1.0, 6.0, ((0, 32),))
    screened = scatter_about(key_of[1], (NG, NG), NG ** -0.5, 0.09375, ((0, 32), (1, 32)))
    poles = jnp.clip(jnp.exp(math.log(4.0) - 2.0794415 * jax.random.uniform(key_of[2], (NG, NG), jnp.float32) ** block_scale(key_of[2], (NG, NG), ((0, 32), (1, 32)), -0.2, 0.2)), 0.5, 4.0).astype(jnp.bfloat16)
    gap_energy = jnp.clip(jnp.exp(jax.random.uniform(key_of[3], (CLASSES,), jnp.float32, math.log(0.3), math.log(3.0))), 0.3, 3.0)
    gap_class = touch_ends(jax.random.randint(key_of[4], (NB, S), 0, CLASSES), jax.random.fold_in(key_of[4], 1), 0, CLASSES - 1).astype(jnp.int32)
    return dict(intersections=intersections, screened=screened, poles=poles, gap_energy=gap_energy, gap_class=gap_class)


def reference(intersections, screened, poles, gap_energy, gap_class):
    amps = screened.astype(jnp.float32)
    freqs = poles.astype(jnp.float32)
    factors = []
    for class_id in range(CLASSES):
        energy = gap_energy[class_id]
        value = amps * freqs / (freqs * freqs + energy * energy)
        factors.append(value.astype(jnp.bfloat16).astype(jnp.float32))

    def one_band(carry, inputs):
        band_rows, band_class = inputs
        left = band_rows.astype(jnp.float32)
        side = jnp.zeros((S, NG), jnp.float32)
        for class_id in range(CLASSES):
            term = lax.dot_general(left, factors[class_id], (((0,), (0,)), ((), ())), precision=lax.Precision.HIGHEST, preferred_element_type=jnp.float32)
            picked = (band_class == class_id).astype(jnp.float32)
            side = side + picked[:, None] * term
        rounded = side.astype(jnp.bfloat16).astype(jnp.float32)
        return (carry + jnp.dot(rounded, left, precision=lax.Precision.HIGHEST, preferred_element_type=jnp.float32), None)
    total, _ = lax.scan(one_band, jnp.zeros((S, S), jnp.float32), (intersections, gap_class))
    return total / jnp.sqrt(jnp.float32(NG * NB))
```

```python
import jax
import jax.numpy as jnp
from jax import lax
from jax.experimental import pallas as pl
from jax.experimental.pallas import tpu as pltpu
from jax.sharding import Mesh, PartitionSpec as P

CLASSES = 3
F32 = jnp.float32
BF16 = jnp.bfloat16


def body(place, energy, y_ref, z_ref, cy_ref, cz_ref, inter_ref, right_ref, class_ref, keep_ref, send_ref, side_acc, full):
    step = pl.program_id(0)
    bands, blocks, size, states = inter_ref.shape
    squares = [energy[c] * energy[c] for c in range(CLASSES)]

    @pl.when(step == 0)
    def _():
        side_acc[...] = jnp.zeros_like(side_acc)

    def add(group):
        half = lax.rem(step, 2) * blocks
        columns = [[] for _ in range(CLASSES)]
        for j in range(blocks):
            amps = group[half + j, 0].astype(F32)
            freqs = group[half + j, 1].astype(F32)
            square = freqs * freqs
            d0, d1, d2 = (square + e for e in squares)
            d12 = d1 * d2
            ratio = amps * freqs / (d0 * d12)
            r0 = ratio * d0
            columns[0].append((ratio * d12).astype(BF16))
            columns[1].append((r0 * d2).astype(BF16))
            columns[2].append((r0 * d1).astype(BF16))
        factor = jnp.concatenate([jnp.concatenate(c, axis=1) for c in columns], axis=0)
        for b in range(bands):
            rows = inter_ref[b].reshape(blocks * size, states)
            side_acc[b] += jnp.dot(factor, rows, preferred_element_type=F32)

    for k, group in enumerate((y_ref, cy_ref, z_ref, cz_ref)):
        pl.when(step // 2 == k)(lambda group=group: add(group))

    @pl.when(step == pl.num_programs(0) - 1)
    def _():
        sides = []
        for b in range(bands):
            kind = class_ref[b : b + 1, :]
            side = jnp.zeros((size, states), F32)
            for c in range(CLASSES):
                side = jnp.where(kind == c, side_acc[b, c * size : (c + 1) * size, :], side)
            sides.append(side.astype(BF16))
        left = jnp.concatenate(sides, axis=0)
        right = right_ref[...].reshape(bands * size, states)
        total = lax.dot_general(left, right, (((0,), (0,)), ((), ())), preferred_element_type=F32)
        full[...] = total.reshape(full.shape)
        core = place[1]
        keep_ref[...] = full[:, core]
        send_ref[...] = full[:, 1 - core]


def terms(place, gap_energy, groups, intersections, gap_class):
    bands, rows, states = intersections.shape
    size = groups[0].shape[-1]
    per = rows // (2 * 2 * size)
    blocks = per // 2
    split = intersections.reshape(bands, 2, per, 2, size, states)
    flat = intersections.reshape(bands, rows // size, size, states)

    def rows_of(t, place):
        k = t // 2
        return (0, (place[0] + k // 2) % 2, t % 2, (place[1] + k % 2) % 2, 0, 0)

    whole = pl.BlockSpec(groups[0].shape, lambda t, place: (0, 0, 0, 0))
    fine = 16
    outer = states // (2 * fine)
    half = jax.ShapeDtypeStruct((outer, fine, states), F32)
    return pl.pallas_call(
        body,
        out_shape=(half, half),
        grid_spec=pltpu.PrefetchScalarGridSpec(
            num_scalar_prefetch=1,
            grid=(8,),
            in_specs=[
                pl.BlockSpec(memory_space=pltpu.SMEM),
                whole,
                whole,
                whole,
                whole,
                pl.BlockSpec((bands, None, blocks, None, size, states), rows_of),
                pl.BlockSpec((bands, None, size, states), lambda t, place: (0, place[2], 0, 0)),
                pl.BlockSpec(gap_class.shape, lambda t, place: (0, 0)),
            ],
            out_specs=[pl.BlockSpec(half.shape, lambda t, place: (0, 0, 0))] * 2,
            scratch_shapes=[
                pltpu.VMEM((bands, CLASSES * size, states), F32),
                pltpu.VMEM((outer, 2, fine, states), F32),
            ],
        ),
        compiler_params=pltpu.CompilerParams(dimension_semantics=("arbitrary",), vmem_limit_bytes=50 << 20),
        cost_estimate=pl.CostEstimate(flops=3 << 30, bytes_accessed=12 << 20, transcendentals=0),
        name="terms",
    )(place, gap_energy, *groups, split, flat, gap_class)


def local(intersections, screened, poles, gap_energy, gap_class):
    zl, y, c = lax.axis_index("zl"), lax.axis_index("y"), lax.axis_index("c")
    column = lax.axis_index("zh") * lax.axis_size("x") + lax.axis_index("x")
    place = jnp.stack([zl, c, column]).astype(jnp.int32)
    swap = [(0, 1), (1, 0)]
    own = jnp.stack([screened.T, poles.T])
    per = lax.axis_size("y")
    y_group = lax.all_to_all(jnp.broadcast_to(own[None], (per,) + own.shape), "y", 0, 0, tiled=True)
    z_group = lax.ppermute(y_group, "zl", swap)
    cy_group = lax.ppermute(y_group, "c", swap)
    cz_group = lax.ppermute(z_group, "c", swap)
    keep, send = terms(place, gap_energy, (y_group, z_group, cy_group, cz_group), intersections, gap_class)
    chip = keep + lax.ppermute(send, "c", swap)
    pieces = lax.all_to_all(chip.astype(BF16), ("zl", "y"), 0, 0, tiled=True)
    rows = jnp.sum(pieces.astype(F32), axis=0)
    columns = lax.axis_size("zh") * lax.axis_size("x")
    fine = rows.shape[0]
    split = rows.reshape(fine, columns, -1).transpose(1, 0, 2)
    wide = split.shape[2]
    blocks = lax.all_to_all(split.reshape(columns, fine * wide), ("zh", "x"), 0, 0, tiled=True)
    total = jnp.sum(blocks, axis=0).reshape(fine, wide)
    count = intersections.shape[1] * intersections.shape[0] * 2 * per * 2
    return total * (1.0 / jnp.sqrt(F32(count)))


def solution(mesh):
    fine = Mesh(mesh.devices.reshape(2, 8, 2, 4, 8), ("zl", "y", "c", "zh", "x"))
    band, col = ("zl", "y", "c"), ("zh", "x")
    return jax.shard_map(
        local,
        mesh=fine,
        in_specs=(P(band, None, None), P(band, col), P(band, col), P(), P(band, None)),
        out_specs=P(band, col),
        check_vma=False,
    )
```

```python
import jax
import jax.numpy as jnp
from jax import lax
from jax.experimental import pallas as pl
from jax.experimental.pallas import tpu as pltpu
from jax.sharding import Mesh, PartitionSpec as P


CLASSES = 3
FINE = 16
F32 = jnp.float32
BF16 = jnp.bfloat16
VMEM = pl.BlockSpec(memory_space=pltpu.VMEM)


def prepare_body(energy, amps_ref, freqs_ref, class_ref, own_ref, square_ref, kind_ref):
    amps = amps_ref[...].astype(F32).T.astype(BF16)
    freqs = freqs_ref[...].astype(F32).T.astype(BF16)
    for k in range(own_ref.shape[0]):
        own_ref[k, 0] = amps
        own_ref[k, 1] = freqs
    for c in range(CLASSES):
        square_ref[c] = jnp.full(square_ref.shape[1:], energy[c] * energy[c], F32)
    kind_ref[...] = class_ref[...]


def prepare(screened, poles, gap_energy, gap_class, copies):
    rows, columns = screened.shape
    return pl.pallas_call(
        prepare_body,
        out_shape=(
            jax.ShapeDtypeStruct((copies, 2, columns, rows), BF16),
            jax.ShapeDtypeStruct((CLASSES, 8, rows), F32),
            jax.ShapeDtypeStruct(gap_class.shape, jnp.int32),
        ),
        grid=(1,),
        in_specs=[
            pl.BlockSpec(memory_space=pltpu.SMEM),
            pl.BlockSpec(screened.shape, lambda t: (0, 0)),
            pl.BlockSpec(poles.shape, lambda t: (0, 0)),
            pl.BlockSpec(gap_class.shape, lambda t: (0, 0)),
        ],
        out_specs=(VMEM, VMEM, VMEM),
        compiler_params=pltpu.CompilerParams(vmem_limit_bytes=8 << 20),
        name="prepare",
    )(*(pltpu.with_memory_space_constraint(a, pltpu.HBM) for a in (gap_energy, screened, poles, gap_class)))


def add_block(group, start, square_ref, inter_ref, acc):
    bands, blocks, size, states = inter_ref.shape
    squares = [square_ref[c, 0:1, :] for c in range(CLASSES)]
    columns = [[] for _ in range(CLASSES)]
    for j in range(blocks):
        amps = group[start + j, 0].astype(F32)
        freqs = group[start + j, 1].astype(F32)
        square = freqs * freqs
        d0, d1, d2 = (square + e for e in squares)
        d12 = d1 * d2
        ratio = amps * freqs / (d0 * d12)
        r0 = ratio * d0
        columns[0].append((ratio * d12).astype(BF16))
        columns[1].append((r0 * d2).astype(BF16))
        columns[2].append((r0 * d1).astype(BF16))
    factor = jnp.concatenate([jnp.concatenate(c, axis=1) for c in columns], axis=0)
    for b in range(bands):
        rows = inter_ref[b].reshape(blocks * size, states)
        acc[b] += jnp.dot(factor, rows, preferred_element_type=F32)


def first_body(place, square_ref, y_ref, cy_ref, inter_ref, acc):
    step = pl.program_id(0)
    start = lax.rem(step, 2) * inter_ref.shape[1]

    @pl.when(step == 0)
    def _():
        acc[...] = jnp.zeros_like(acc)

    pl.when(step // 2 == 0)(lambda: add_block(y_ref, start, square_ref, inter_ref, acc))
    pl.when(step // 2 == 1)(lambda: add_block(cy_ref, start, square_ref, inter_ref, acc))


def second_body(place, square_ref, z_ref, inter_ref, acc_in, acc):
    @pl.when(pl.program_id(0) == 0)
    def _():
        acc[...] = acc_in[...]

    add_block(z_ref, pl.program_id(0) * inter_ref.shape[1], square_ref, inter_ref, acc)


def third_body(place, square_ref, kind_ref, cz_ref, inter_ref, right_ref, acc_in, keep_ref, send_ref, acc, full):
    step = pl.program_id(0)
    bands, _, size, states = inter_ref.shape

    @pl.when(step == 0)
    def _():
        acc[...] = acc_in[...]

    add_block(cz_ref, step * inter_ref.shape[1], square_ref, inter_ref, acc)

    @pl.when(step == pl.num_programs(0) - 1)
    def _():
        sides = []
        for b in range(bands):
            kind = kind_ref[b : b + 1, :]
            side = jnp.zeros((size, states), F32)
            for c in range(CLASSES):
                side = jnp.where(kind == c, acc[b, c * size : (c + 1) * size, :], side)
            sides.append(side.astype(BF16))
        left = jnp.concatenate(sides, axis=0)
        right = right_ref[...].reshape(bands * size, states)
        total = lax.dot_general(left, right, (((0,), (0,)), ((), ())), preferred_element_type=F32)
        full[...] = total.reshape(full.shape)
        core = place[1]
        keep_ref[...] = full[:, core]
        send_ref[...] = full[:, 1 - core]


class Terms:
    def __init__(self, place, square, kind, intersections, per, size):
        bands, rows, states = intersections.shape
        self.place, self.square, self.kind = place, square, kind
        self.split = intersections.reshape(bands, 2, per, 2, size, states)
        self.flat = intersections.reshape(bands, rows // size, size, states)
        self.blocks = per // 2
        self.size = size
        self.acc = jax.ShapeDtypeStruct((bands, CLASSES * size, states), F32)

    def rows_spec(self, other_z, other_core):
        bands, _, _, _, size, states = self.split.shape

        def index(t, place):
            c = place[1] if other_core == 0 else 1 - place[1]
            c = c if other_core < 2 else lax.rem(place[1] + t // 2, 2)
            return (0, lax.rem(place[0] + other_z, 2), lax.rem(t, 2), c, 0, 0)

        return pl.BlockSpec((bands, None, self.blocks, None, size, states), index)

    def call(self, body, steps, operands, specs, out_shape, scratch=()):
        flops = 2 * self.acc.shape[0] * self.acc.shape[1] * self.acc.shape[2] * steps * self.blocks * self.size
        return pl.pallas_call(
            body,
            out_shape=out_shape,
            grid_spec=pltpu.PrefetchScalarGridSpec(
                num_scalar_prefetch=1,
                grid=(steps,),
                in_specs=specs,
                out_specs=VMEM if not isinstance(out_shape, tuple) else tuple(VMEM for _ in out_shape),
                scratch_shapes=scratch,
            ),
            compiler_params=pltpu.CompilerParams(dimension_semantics=("arbitrary",), vmem_limit_bytes=50 << 20),
            cost_estimate=pl.CostEstimate(flops=flops, bytes_accessed=steps << 20, transcendentals=0),
        )(self.place, *operands)

    def first(self, y_group, cy_group):
        return self.call(
            first_body, 4,
            (self.square, y_group, cy_group, self.split),
            [VMEM, VMEM, VMEM, self.rows_spec(0, 2)],
            self.acc,
        )

    def second(self, z_group, acc):
        return self.call(
            second_body, 2,
            (self.square, z_group, self.split, acc),
            [VMEM, VMEM, self.rows_spec(1, 0), VMEM],
            self.acc,
        )

    def third(self, cz_group, acc):
        bands, size, states = acc.shape[0], self.size, acc.shape[2]
        outer = states // (2 * FINE)
        half = jax.ShapeDtypeStruct((outer, FINE, states), F32)
        right = pl.BlockSpec((bands, None, size, states), lambda t, place: (0, place[2], 0, 0))
        return self.call(
            third_body, 2,
            (self.square, self.kind, cz_group, self.split, self.flat, acc),
            [VMEM, VMEM, VMEM, self.rows_spec(1, 1), right, VMEM],
            (half, half),
            [pltpu.VMEM(self.acc.shape, F32), pltpu.VMEM((outer, 2, FINE, states), F32)],
        )


def local(intersections, screened, poles, gap_energy, gap_class):
    zl, c = lax.axis_index("zl"), lax.axis_index("c")
    column = lax.axis_index("zh") * lax.axis_size("x") + lax.axis_index("x")
    place = jnp.stack([zl, c, column]).astype(jnp.int32)
    swap = [(0, 1), (1, 0)]
    per = lax.axis_size("y")
    own, square, kind = prepare(screened, poles, gap_energy, gap_class, per)
    terms = Terms(place, square, kind, intersections, per, screened.shape[0])
    y_group = lax.all_to_all(own, "y", 0, 0, tiled=True)
    z_group = lax.ppermute(y_group, "zl", swap)
    cy_group = lax.ppermute(y_group, "c", swap)
    acc = terms.first(y_group, cy_group)
    cz_group = lax.ppermute(z_group, "c", swap)
    acc = terms.second(z_group, acc)
    keep, send = terms.third(cz_group, acc)
    chip = keep + lax.ppermute(send, "c", swap)
    pieces = lax.all_to_all(chip.astype(BF16), ("zl", "y"), 0, 0, tiled=True)
    rows = jnp.sum(pieces.astype(F32), axis=0)
    columns = lax.axis_size("zh") * lax.axis_size("x")
    fine = rows.shape[0]
    split = rows.reshape(fine, columns, -1).transpose(1, 0, 2)
    wide = split.shape[2]
    blocks = lax.all_to_all(split.reshape(columns, fine * wide), ("zh", "x"), 0, 0, tiled=True)
    total = jnp.sum(blocks, axis=0).reshape(fine, wide)
    count = intersections.shape[1] * intersections.shape[0] * 2 * per * 2
    return total * (1.0 / jnp.sqrt(F32(count)))


def solution(mesh):
    fine = Mesh(mesh.devices.reshape(2, 8, 2, 4, 8), ("zl", "y", "c", "zh", "x"))
    band, col = ("zl", "y", "c"), ("zh", "x")
    return jax.shard_map(
        local,
        mesh=fine,
        in_specs=(P(band, None, None), P(band, col), P(band, col), P(), P(band, None)),
        out_specs=P(band, col),
        check_vma=False,
    )
```

```python
import jax
import jax.numpy as jnp
from jax import lax
from jax.experimental import pallas as pl
from jax.experimental.pallas import tpu as pltpu
from jax.sharding import Mesh, PartitionSpec as P


CLASSES = 3
FINE = 16
LIMIT = 32 << 20
F32 = jnp.float32
BF16 = jnp.bfloat16
VMEM = pl.BlockSpec(memory_space=pltpu.VMEM)


def prepare_body(energy, amps_ref, freqs_ref, class_ref, own_ref, square_ref, kind_ref):
    amps = amps_ref[...].astype(F32).T.astype(BF16)
    freqs = freqs_ref[...].astype(F32).T.astype(BF16)
    for k in range(own_ref.shape[0]):
        own_ref[k, 0] = amps
        own_ref[k, 1] = freqs
    for c in range(CLASSES):
        square_ref[c] = jnp.full(square_ref.shape[1:], energy[c] * energy[c], F32)
    kind_ref[...] = class_ref[...]


def prepare(screened, poles, gap_energy, gap_class, copies):
    rows, columns = screened.shape
    return pl.pallas_call(
        prepare_body,
        out_shape=(
            jax.ShapeDtypeStruct((copies, 2, columns, rows), BF16),
            jax.ShapeDtypeStruct((CLASSES, 8, rows), F32),
            jax.ShapeDtypeStruct(gap_class.shape, jnp.int32),
        ),
        grid=(1,),
        in_specs=[
            pl.BlockSpec(memory_space=pltpu.SMEM),
            pl.BlockSpec(screened.shape, lambda t: (0, 0)),
            pl.BlockSpec(poles.shape, lambda t: (0, 0)),
            pl.BlockSpec(gap_class.shape, lambda t: (0, 0)),
        ],
        out_specs=(VMEM, VMEM, VMEM),
        compiler_params=pltpu.CompilerParams(vmem_limit_bytes=8 << 20),
        name="prepare",
    )(*(pltpu.with_memory_space_constraint(a, pltpu.HBM) for a in (gap_energy, screened, poles, gap_class)))


def factors(group, start, blocks, square_ref):
    squares = [square_ref[c, 0:1, :] for c in range(CLASSES)]
    columns = [[] for _ in range(CLASSES)]
    for j in range(blocks):
        amps = group[start + j, 0].astype(F32)
        freqs = group[start + j, 1].astype(F32)
        square = freqs * freqs
        d0, d1, d2 = (square + e for e in squares)
        d12 = d1 * d2
        ratio = amps * freqs / (d0 * d12)
        r0 = ratio * d0
        columns[0].append((ratio * d12).astype(BF16))
        columns[1].append((r0 * d2).astype(BF16))
        columns[2].append((r0 * d1).astype(BF16))
    return jnp.concatenate([jnp.concatenate(c, axis=1) for c in columns], axis=0)


def first_body(place, square_ref, y_ref, cy_ref, inter_ref, split_ref, flat_ref, acc, same_ref, cross_ref, right_ref, sems):
    step = pl.program_id(0)
    bands, blocks, size, states = inter_ref.shape
    other_z, core = 1 - place[0], place[1]
    copies = [
        pltpu.make_async_copy(split_ref.at[:, other_z, :, core], same_ref, sems.at[0]),
        pltpu.make_async_copy(split_ref.at[:, other_z, :, 1 - core], cross_ref, sems.at[1]),
        pltpu.make_async_copy(flat_ref.at[:, place[2]], right_ref, sems.at[2]),
    ]

    @pl.when(step == 0)
    def _():
        acc[...] = jnp.zeros_like(acc)

    @pl.when(step == 1)
    def _():
        for copy in copies:
            copy.start()

    def add(group):
        factor = factors(group, lax.rem(step, 2) * blocks, blocks, square_ref)
        for b in range(bands):
            rows = inter_ref[b].reshape(blocks * size, states)
            acc[b] += jnp.dot(factor, rows, preferred_element_type=F32)

    pl.when(step // 2 == 0)(lambda: add(y_ref))
    pl.when(step // 2 == 1)(lambda: add(cy_ref))

    @pl.when(step == pl.num_programs(0) - 1)
    def _():
        for copy in copies:
            copy.wait()


def second_body(square_ref, z_ref, inter_ref, acc_in, acc):
    bands, blocks, size, states = inter_ref.shape
    factor = factors(z_ref, 0, blocks, square_ref)
    for b in range(bands):
        rows = inter_ref[b].reshape(blocks * size, states)
        acc[b] = acc_in[b] + jnp.dot(factor, rows, preferred_element_type=F32)


def third_body(square_ref, kind_ref, cz_ref, inter_ref, right_ref, acc_in, keep_ref, send_ref, full):
    bands, blocks, size, states = inter_ref.shape
    factor = factors(cz_ref, 0, blocks, square_ref)
    sides = []
    for b in range(bands):
        rows = inter_ref[b].reshape(blocks * size, states)
        acc = acc_in[b] + jnp.dot(factor, rows, preferred_element_type=F32)
        kind = kind_ref[b : b + 1, :]
        side = jnp.zeros((size, states), F32)
        for c in range(CLASSES):
            side = jnp.where(kind == c, acc[c * size : (c + 1) * size, :], side)
        sides.append(side.astype(BF16))
    left = jnp.concatenate(sides, axis=0)
    right = right_ref[...].reshape(bands * size, states)
    total = lax.dot_general(left, right, (((0,), (0,)), ((), ())), preferred_element_type=F32)
    full[...] = total.reshape(full.shape)
    core = lax.axis_index("c")
    keep_ref[...] = full[:, core]
    send_ref[...] = full[:, 1 - core]


def work(acc, blocks, size, steps):
    flops = 2 * acc.shape[0] * acc.shape[1] * acc.shape[2] * blocks * size * steps
    return pl.CostEstimate(flops=flops, bytes_accessed=1 << 20, transcendentals=0)


def first(place, square, y_group, cy_group, intersections):
    bands, rows, states = intersections.shape
    per, size = y_group.shape[0], y_group.shape[3]
    blocks = per // 2
    split = pltpu.with_memory_space_constraint(intersections.reshape(bands, 2, per, 2, size, states), pltpu.HBM)
    flat = pltpu.with_memory_space_constraint(intersections.reshape(bands, rows // size, size, states), pltpu.HBM)
    acc = jax.ShapeDtypeStruct((bands, CLASSES * size, states), F32)
    half = jax.ShapeDtypeStruct((bands, per, size, states), BF16)
    right = jax.ShapeDtypeStruct((bands, size, states), BF16)

    def rows_of(t, place):
        return (0, place[0], lax.rem(t, 2), lax.rem(place[1] + t // 2, 2), 0, 0)

    return pl.pallas_call(
        first_body,
        out_shape=(acc, half, half, right),
        grid_spec=pltpu.PrefetchScalarGridSpec(
            num_scalar_prefetch=1,
            grid=(4,),
            in_specs=[
                VMEM,
                VMEM,
                VMEM,
                pl.BlockSpec((bands, None, blocks, None, size, states), rows_of),
                pl.BlockSpec(memory_space=pltpu.HBM),
                pl.BlockSpec(memory_space=pltpu.HBM),
            ],
            out_specs=(VMEM,) * 4,
            scratch_shapes=[pltpu.SemaphoreType.DMA((3,))],
        ),
        compiler_params=pltpu.CompilerParams(dimension_semantics=("arbitrary",), vmem_limit_bytes=LIMIT),
        cost_estimate=work(acc, blocks, size, 4),
        name="first",
    )(place, square, y_group, cy_group, split, split, flat)


def second(square, z_group, inter, acc):
    return pl.pallas_call(
        second_body,
        out_shape=jax.ShapeDtypeStruct(acc.shape, F32),
        in_specs=[VMEM] * 4,
        out_specs=VMEM,
        compiler_params=pltpu.CompilerParams(vmem_limit_bytes=LIMIT),
        cost_estimate=work(acc, *inter.shape[1:3], 1),
        name="second",
    )(square, z_group, inter, acc)


def third(square, kind, cz_group, inter, right, acc):
    outer, states = acc.shape[2] // (2 * FINE), acc.shape[2]
    half = jax.ShapeDtypeStruct((outer, FINE, states), F32)
    return pl.pallas_call(
        third_body,
        out_shape=(half, half),
        in_specs=[VMEM] * 6,
        out_specs=(VMEM, VMEM),
        scratch_shapes=[pltpu.VMEM((outer, 2, FINE, states), F32)],
        compiler_params=pltpu.CompilerParams(vmem_limit_bytes=LIMIT),
        cost_estimate=work(acc, *inter.shape[1:3], 1),
        name="third",
    )(square, kind, cz_group, inter, right, acc)


def local(intersections, screened, poles, gap_energy, gap_class):
    zl, c = lax.axis_index("zl"), lax.axis_index("c")
    column = lax.axis_index("zh") * lax.axis_size("x") + lax.axis_index("x")
    place = jnp.stack([zl, c, column]).astype(jnp.int32)
    swap = [(0, 1), (1, 0)]
    per = lax.axis_size("y")
    own, square, kind = prepare(screened, poles, gap_energy, gap_class, per)
    y_group = lax.all_to_all(own, "y", 0, 0, tiled=True)
    z_group = lax.ppermute(y_group, "zl", swap)
    cy_group = lax.ppermute(y_group, "c", swap)
    acc, same, cross, right = first(place, square, y_group, cy_group, intersections)
    cz_group = lax.ppermute(z_group, "c", swap)
    acc = second(square, z_group, same, acc)
    keep, send = third(square, kind, cz_group, cross, right, acc)
    chip = keep + lax.ppermute(send, "c", swap)
    pieces = lax.all_to_all(chip.astype(BF16), ("zl", "y"), 0, 0, tiled=True)
    rows = jnp.sum(pieces.astype(F32), axis=0)
    columns = lax.axis_size("zh") * lax.axis_size("x")
    fine = rows.shape[0]
    split = rows.reshape(fine, columns, -1).transpose(1, 0, 2)
    wide = split.shape[2]
    blocks = lax.all_to_all(split.reshape(columns, fine * wide), ("zh", "x"), 0, 0, tiled=True)
    total = jnp.sum(blocks, axis=0).reshape(fine, wide)
    count = intersections.shape[1] * intersections.shape[0] * 2 * per * 2
    return total * (1.0 / jnp.sqrt(F32(count)))


def solution(mesh):
    fine = Mesh(mesh.devices.reshape(2, 8, 2, 4, 8), ("zl", "y", "c", "zh", "x"))
    band, col = ("zl", "y", "c"), ("zh", "x")
    return jax.shard_map(
        local,
        mesh=fine,
        in_specs=(P(band, None, None), P(band, col), P(band, col), P(), P(band, None)),
        out_specs=P(band, col),
        check_vma=False,
    )
```

```python
import jax
import jax.numpy as jnp
from jax import lax
from jax.experimental import pallas as pl
from jax.experimental.pallas import tpu as pltpu
from jax.sharding import Mesh, PartitionSpec as P


CLASSES = 3
FINE = 16
LIMIT = 32 << 20
F32 = jnp.float32
BF16 = jnp.bfloat16
VMEM = pl.BlockSpec(memory_space=pltpu.VMEM)


def prepare_body(energy, amps_ref, freqs_ref, class_ref, own_ref, square_ref, kind_ref):
    amps = amps_ref[...].astype(F32).T.astype(BF16)
    freqs = freqs_ref[...].astype(F32).T.astype(BF16)
    for k in range(own_ref.shape[0]):
        own_ref[k, 0] = amps
        own_ref[k, 1] = freqs
    for c in range(CLASSES):
        square_ref[c] = jnp.full(square_ref.shape[1:], energy[c] * energy[c], F32)
    kind_ref[...] = class_ref[...]


def prepare(screened, poles, gap_energy, gap_class, copies):
    rows, columns = screened.shape
    return pl.pallas_call(
        prepare_body,
        out_shape=(
            jax.ShapeDtypeStruct((copies, 2, columns, rows), BF16),
            jax.ShapeDtypeStruct((CLASSES, 8, rows), F32),
            jax.ShapeDtypeStruct(gap_class.shape, jnp.int32),
        ),
        grid=(1,),
        in_specs=[
            pl.BlockSpec(memory_space=pltpu.SMEM),
            pl.BlockSpec(screened.shape, lambda t: (0, 0)),
            pl.BlockSpec(poles.shape, lambda t: (0, 0)),
            pl.BlockSpec(gap_class.shape, lambda t: (0, 0)),
        ],
        out_specs=(VMEM, VMEM, VMEM),
        compiler_params=pltpu.CompilerParams(vmem_limit_bytes=8 << 20),
        name="prepare",
    )(*(pltpu.with_memory_space_constraint(a, pltpu.HBM) for a in (gap_energy, screened, poles, gap_class)))


def factors(group, start, blocks, square_ref):
    squares = [square_ref[c, 0:1, :] for c in range(CLASSES)]
    columns = [[] for _ in range(CLASSES)]
    for j in range(blocks):
        amps = group[start + j, 0].astype(F32)
        freqs = group[start + j, 1].astype(F32)
        square = freqs * freqs
        d0, d1, d2 = (square + e for e in squares)
        d12 = d1 * d2
        ratio = amps * freqs / (d0 * d12)
        r0 = ratio * d0
        columns[0].append((ratio * d12).astype(BF16))
        columns[1].append((r0 * d2).astype(BF16))
        columns[2].append((r0 * d1).astype(BF16))
    return jnp.concatenate([jnp.concatenate(c, axis=1) for c in columns], axis=0)


def first_body(place, square_ref, y_ref, inter_ref, split_ref, flat_ref, acc, near_ref, same_ref, cross_ref, right_ref, sems):
    step = pl.program_id(0)
    bands, blocks, size, states = inter_ref.shape
    own_z, core = place[0], place[1]
    half = size // 2
    copies = [
        pltpu.make_async_copy(split_ref.at[:, own_z, :, 1 - core], near_ref, sems.at[0]),
        pltpu.make_async_copy(split_ref.at[:, 1 - own_z, :, core], same_ref, sems.at[1]),
        pltpu.make_async_copy(split_ref.at[:, 1 - own_z, :, 1 - core], cross_ref, sems.at[2]),
        pltpu.make_async_copy(flat_ref.at[:, place[2]], right_ref.at[:, :size], sems.at[3]),
        pltpu.make_async_copy(flat_ref.at[:, place[3], half:], right_ref.at[:, size:], sems.at[4]),
    ]

    @pl.when(step == 0)
    def _():
        for copy in copies:
            copy.start()
        acc[...] = jnp.zeros_like(acc)

    factor = factors(y_ref, step * blocks, blocks, square_ref)
    for b in range(bands):
        rows = inter_ref[b].reshape(blocks * size, states)
        acc[b] += jnp.dot(factor, rows, preferred_element_type=F32)

    @pl.when(step == pl.num_programs(0) - 1)
    def _():
        for copy in copies:
            copy.wait()


def second_body(square_ref, cy_ref, zd_ref, zo_ref, near_ref, same_ref, acc_in, acc, far):
    bands, blocks, size, states = near_ref.shape
    factor = factors(cy_ref, 0, blocks, square_ref)
    cross = jnp.concatenate([factors(zd_ref, 0, blocks, square_ref), factors(zo_ref, 0, blocks, square_ref)], axis=0)
    for b in range(bands):
        rows = near_ref[b].reshape(blocks * size, states)
        acc[b] = acc_in[b] + jnp.dot(factor, rows, preferred_element_type=F32)
        rows = same_ref[b].reshape(blocks * size, states)
        far[b] = jnp.dot(cross, rows, preferred_element_type=F32)


def chosen(kind, terms):
    side = jnp.zeros_like(terms[0])
    for c in range(CLASSES):
        side = jnp.where(kind == c, terms[c], side)
    return side.astype(BF16)


def third_body(square_ref, kind_ref, czd_ref, czo_ref, cross_ref, right_ref, acc, far_in, keep_ref, send_ref, full):
    bands, blocks, size, states = cross_ref.shape
    half = size // 2
    cross = jnp.concatenate([factors(czd_ref, 0, blocks, square_ref), factors(czo_ref, 0, blocks, square_ref)], axis=0)
    sides = []
    for b in range(bands):
        rows = cross_ref[b].reshape(blocks * size, states)
        far = far_in[b] + jnp.dot(cross, rows, preferred_element_type=F32)
        kind = kind_ref[b : b + 1, :]
        low = [acc[b, c * size : c * size + half, :] + far[c * half : (c + 1) * half, :] for c in range(CLASSES)]
        high = [acc[b, c * size + half : (c + 1) * size, :] for c in range(CLASSES)]
        away = [far[(CLASSES + c) * half : (CLASSES + c + 1) * half, :] for c in range(CLASSES)]
        sides += [chosen(kind, low), chosen(kind, high), chosen(kind, away)]
    left = jnp.concatenate(sides, axis=0)
    right = right_ref[...].reshape(bands * (size + half), states)
    total = lax.dot_general(left, right, (((0,), (0,)), ((), ())), preferred_element_type=F32)
    full[...] = total.reshape(full.shape)
    core = lax.axis_index("c")
    keep_ref[...] = full[:, core]
    send_ref[...] = full[:, 1 - core]


def work(acc, blocks, size, steps):
    flops = 2 * acc.shape[0] * acc.shape[1] * acc.shape[2] * blocks * size * steps
    return pl.CostEstimate(flops=flops, bytes_accessed=1 << 20, transcendentals=0)


def first(place, square, y_group, intersections):
    bands, rows, states = intersections.shape
    per, size = y_group.shape[0], y_group.shape[3]
    blocks = per // 2
    split = pltpu.with_memory_space_constraint(intersections.reshape(bands, 2, per, 2, size, states), pltpu.HBM)
    flat = pltpu.with_memory_space_constraint(intersections.reshape(bands, rows // size, size, states), pltpu.HBM)
    acc = jax.ShapeDtypeStruct((bands, CLASSES * size, states), F32)
    part = jax.ShapeDtypeStruct((bands, per, size, states), BF16)
    right = jax.ShapeDtypeStruct((bands, size + size // 2, states), BF16)
    return pl.pallas_call(
        first_body,
        out_shape=(acc, part, part, part, right),
        grid_spec=pltpu.PrefetchScalarGridSpec(
            num_scalar_prefetch=1,
            grid=(2,),
            in_specs=[
                VMEM,
                VMEM,
                pl.BlockSpec((bands, None, blocks, None, size, states), lambda t, place: (0, place[0], t, place[1], 0, 0)),
                pl.BlockSpec(memory_space=pltpu.HBM),
                pl.BlockSpec(memory_space=pltpu.HBM),
            ],
            out_specs=(VMEM,) * 5,
            scratch_shapes=[pltpu.SemaphoreType.DMA((5,))],
        ),
        compiler_params=pltpu.CompilerParams(dimension_semantics=("arbitrary",), vmem_limit_bytes=LIMIT),
        cost_estimate=work(acc, blocks, size, 2),
        name="first",
    )(place, square, y_group, split, split, flat)


def second(square, cy_group, zd_group, zo_group, near, same, acc):
    shape = jax.ShapeDtypeStruct(acc.shape, F32)
    return pl.pallas_call(
        second_body,
        out_shape=(shape, shape),
        in_specs=[VMEM] * 7,
        out_specs=(VMEM, VMEM),
        compiler_params=pltpu.CompilerParams(vmem_limit_bytes=LIMIT),
        cost_estimate=work(acc, *near.shape[1:3], 2),
        name="second",
    )(square, cy_group, zd_group, zo_group, near, same, acc)


def third(square, kind, czd_group, czo_group, cross, right, acc, far):
    outer, states = acc.shape[2] // (2 * FINE), acc.shape[2]
    half = jax.ShapeDtypeStruct((outer, FINE, states), F32)
    return pl.pallas_call(
        third_body,
        out_shape=(half, half),
        in_specs=[VMEM] * 8,
        out_specs=(VMEM, VMEM),
        scratch_shapes=[pltpu.VMEM((outer, 2, FINE, states), F32)],
        compiler_params=pltpu.CompilerParams(vmem_limit_bytes=LIMIT),
        cost_estimate=work(acc, *cross.shape[1:3], 1),
        name="third",
    )(square, kind, czd_group, czo_group, cross, right, acc, far)


def local(intersections, screened, poles, gap_energy, gap_class):
    zl, c = lax.axis_index("zl"), lax.axis_index("c")
    zh, x = lax.axis_index("zh"), lax.axis_index("x")
    along = lax.axis_size("zh")
    beside = lax.rem(zh + jnp.where(zl == 0, along - 1, 1), along)
    place = jnp.stack([zl, c, zh * lax.axis_size("x") + x, beside * lax.axis_size("x") + x]).astype(jnp.int32)
    swap = [(0, 1), (1, 0)]
    aside = [(k, along + (k - 1) % along) for k in range(along)] + [(along + k, (k + 1) % along) for k in range(along)]
    per = lax.axis_size("y")
    own, square, kind = prepare(screened, poles, gap_energy, gap_class, per)
    y_group = lax.all_to_all(own, "y", 0, 0, tiled=True)
    half = y_group.shape[2] // 2
    zd_group = lax.ppermute(y_group[:, :, :half], "zl", swap)
    zo_group = lax.ppermute(y_group[:, :, half:], ("zl", "zh"), aside)
    cy_group = lax.ppermute(y_group, "c", swap)
    acc, near, same, cross, right = first(place, square, y_group, intersections)
    czd_group = lax.ppermute(zd_group, "c", swap)
    czo_group = lax.ppermute(zo_group, "c", swap)
    acc, far = second(square, cy_group, zd_group, zo_group, near, same, acc)
    keep, send = third(square, kind, czd_group, czo_group, cross, right, acc, far)
    chip = keep + lax.ppermute(send, "c", swap)
    pieces = lax.all_to_all(chip.astype(BF16), ("zl", "y"), 0, 0, tiled=True)
    rows = jnp.sum(pieces.astype(F32), axis=0)
    columns = lax.axis_size("zh") * lax.axis_size("x")
    fine = rows.shape[0]
    split = rows.reshape(fine, columns, -1).transpose(1, 0, 2)
    wide = split.shape[2]
    blocks = lax.all_to_all(split.reshape(columns, fine * wide), ("zh", "x"), 0, 0, tiled=True)
    total = jnp.sum(blocks, axis=0).reshape(fine, wide)
    count = intersections.shape[1] * intersections.shape[0] * 2 * per * 2
    return total * (1.0 / jnp.sqrt(F32(count)))


def solution(mesh):
    fine = Mesh(mesh.devices.reshape(2, 8, 2, 4, 8), ("zl", "y", "c", "zh", "x"))
    band, col = ("zl", "y", "c"), ("zh", "x")
    return jax.shard_map(
        local,
        mesh=fine,
        in_specs=(P(band, None, None), P(band, col), P(band, col), P(), P(band, None)),
        out_specs=P(band, col),
        check_vma=False,
    )
```

```python
import jax
import jax.numpy as jnp
from jax import lax
from jax.experimental import pallas as pl
from jax.experimental.pallas import tpu as pltpu
from jax.sharding import Mesh, PartitionSpec as P


CLASSES = 3
FINE = 16
LIMIT = 32 << 20
F32 = jnp.float32
BF16 = jnp.bfloat16
VMEM = pl.BlockSpec(memory_space=pltpu.VMEM)


def prepare_body(energy, amps_ref, freqs_ref, class_ref, own_ref, square_ref, kind_ref):
    amps = amps_ref[...].astype(F32).T.astype(BF16)
    freqs = freqs_ref[...].astype(F32).T.astype(BF16)
    for k in range(own_ref.shape[0]):
        own_ref[k, 0] = amps
        own_ref[k, 1] = freqs
    for c in range(CLASSES):
        square_ref[c] = jnp.full(square_ref.shape[1:], energy[c] * energy[c], F32)
    kind_ref[...] = class_ref[...]


def prepare(screened, poles, gap_energy, gap_class, copies):
    rows, columns = screened.shape
    return pl.pallas_call(
        prepare_body,
        out_shape=(
            jax.ShapeDtypeStruct((copies, 2, columns, rows), BF16),
            jax.ShapeDtypeStruct((CLASSES, 8, rows), F32),
            jax.ShapeDtypeStruct(gap_class.shape, jnp.int32),
        ),
        grid=(1,),
        in_specs=[
            pl.BlockSpec(memory_space=pltpu.SMEM),
            pl.BlockSpec(screened.shape, lambda t: (0, 0)),
            pl.BlockSpec(poles.shape, lambda t: (0, 0)),
            pl.BlockSpec(gap_class.shape, lambda t: (0, 0)),
        ],
        out_specs=(VMEM, VMEM, VMEM),
        compiler_params=pltpu.CompilerParams(vmem_limit_bytes=8 << 20),
        name="prepare",
    )(*(pltpu.with_memory_space_constraint(a, pltpu.HBM) for a in (gap_energy, screened, poles, gap_class)))


def factors(group, start, blocks, square_ref):
    squares = [square_ref[c, 0:1, :] for c in range(CLASSES)]
    columns = [[] for _ in range(CLASSES)]
    for j in range(blocks):
        amps = group[start + j, 0].astype(F32)
        freqs = group[start + j, 1].astype(F32)
        square = freqs * freqs
        d0, d1, d2 = (square + e for e in squares)
        d12 = d1 * d2
        ratio = amps * freqs / (d0 * d12)
        r0 = ratio * d0
        columns[0].append((ratio * d12).astype(BF16))
        columns[1].append((r0 * d2).astype(BF16))
        columns[2].append((r0 * d1).astype(BF16))
    return jnp.concatenate([jnp.concatenate(c, axis=1) for c in columns], axis=0)


def first_body(place, square_ref, y_ref, cy_ref, inter_ref, split_ref, flat_ref, acc, same_ref, cross_ref, right_ref, sems):
    step = pl.program_id(0)
    bands, blocks, size, states = inter_ref.shape
    other_z, core = 1 - place[0], place[1]
    copies = [
        pltpu.make_async_copy(split_ref.at[:, other_z, :, core], same_ref, sems.at[0]),
        pltpu.make_async_copy(split_ref.at[:, other_z, :, 1 - core], cross_ref, sems.at[1]),
        pltpu.make_async_copy(flat_ref.at[:, place[2]], right_ref, sems.at[2]),
    ]

    @pl.when(step == 0)
    def _():
        acc[...] = jnp.zeros_like(acc)

    @pl.when(step == 1)
    def _():
        for copy in copies:
            copy.start()

    def add(group):
        factor = factors(group, lax.rem(step, 2) * blocks, blocks, square_ref)
        for b in range(bands):
            rows = inter_ref[b].reshape(blocks * size, states)
            acc[b] += jnp.dot(factor, rows, preferred_element_type=F32)

    pl.when(step // 2 == 0)(lambda: add(y_ref))
    pl.when(step // 2 == 1)(lambda: add(cy_ref))

    @pl.when(step == pl.num_programs(0) - 1)
    def _():
        for copy in copies:
            copy.wait()


def second_body(square_ref, z_ref, inter_ref, acc_in, acc):
    bands, blocks, size, states = inter_ref.shape
    factor = factors(z_ref, 0, blocks, square_ref)
    for b in range(bands):
        rows = inter_ref[b].reshape(blocks * size, states)
        acc[b] = acc_in[b] + jnp.dot(factor, rows, preferred_element_type=F32)


def third_body(square_ref, kind_ref, cz_ref, inter_ref, right_ref, acc_in, full_ref):
    bands, blocks, size, states = inter_ref.shape
    factor = factors(cz_ref, 0, blocks, square_ref)
    sides = []
    for b in range(bands):
        rows = inter_ref[b].reshape(blocks * size, states)
        acc = acc_in[b] + jnp.dot(factor, rows, preferred_element_type=F32)
        kind = kind_ref[b : b + 1, :]
        side = jnp.zeros((size, states), F32)
        for c in range(CLASSES):
            side = jnp.where(kind == c, acc[c * size : (c + 1) * size, :], side)
        sides.append(side.astype(BF16))
    left = jnp.concatenate(sides, axis=0)
    right = right_ref[...].reshape(bands * size, states)
    total = lax.dot_general(left, right, (((0,), (0,)), ((), ())), preferred_element_type=F32)
    total = total.reshape(full_ref.shape[1], 2, FINE, states)
    full_ref[0] = total[:, 0]
    full_ref[1] = total[:, 1]


def work(acc, blocks, size, steps):
    flops = 2 * acc.shape[0] * acc.shape[1] * acc.shape[2] * blocks * size * steps
    return pl.CostEstimate(flops=flops, bytes_accessed=1 << 20, transcendentals=0)


def first(place, square, y_group, cy_group, intersections):
    bands, rows, states = intersections.shape
    per, size = y_group.shape[0], y_group.shape[3]
    blocks = per // 2
    split = pltpu.with_memory_space_constraint(intersections.reshape(bands, 2, per, 2, size, states), pltpu.HBM)
    flat = pltpu.with_memory_space_constraint(intersections.reshape(bands, rows // size, size, states), pltpu.HBM)
    acc = jax.ShapeDtypeStruct((bands, CLASSES * size, states), F32)
    half = jax.ShapeDtypeStruct((bands, per, size, states), BF16)
    right = jax.ShapeDtypeStruct((bands, size, states), BF16)

    def rows_of(t, place):
        return (0, place[0], lax.rem(t, 2), lax.rem(place[1] + t // 2, 2), 0, 0)

    return pl.pallas_call(
        first_body,
        out_shape=(acc, half, half, right),
        grid_spec=pltpu.PrefetchScalarGridSpec(
            num_scalar_prefetch=1,
            grid=(4,),
            in_specs=[
                VMEM,
                VMEM,
                VMEM,
                pl.BlockSpec((bands, None, blocks, None, size, states), rows_of),
                pl.BlockSpec(memory_space=pltpu.HBM),
                pl.BlockSpec(memory_space=pltpu.HBM),
            ],
            out_specs=(VMEM,) * 4,
            scratch_shapes=[pltpu.SemaphoreType.DMA((3,))],
        ),
        compiler_params=pltpu.CompilerParams(dimension_semantics=("arbitrary",), vmem_limit_bytes=LIMIT),
        cost_estimate=work(acc, blocks, size, 4),
        name="first",
    )(place, square, y_group, cy_group, split, split, flat)


def second(square, z_group, inter, acc):
    return pl.pallas_call(
        second_body,
        out_shape=jax.ShapeDtypeStruct(acc.shape, F32),
        in_specs=[VMEM] * 4,
        out_specs=VMEM,
        compiler_params=pltpu.CompilerParams(vmem_limit_bytes=LIMIT),
        cost_estimate=work(acc, *inter.shape[1:3], 1),
        name="second",
    )(square, z_group, inter, acc)


def third(square, kind, cz_group, inter, right, acc):
    outer, states = acc.shape[2] // (2 * FINE), acc.shape[2]
    return pl.pallas_call(
        third_body,
        out_shape=jax.ShapeDtypeStruct((2, outer, FINE, states), F32),
        in_specs=[VMEM] * 6,
        out_specs=VMEM,
        compiler_params=pltpu.CompilerParams(vmem_limit_bytes=LIMIT),
        cost_estimate=work(acc, *inter.shape[1:3], 1),
        name="third",
    )(square, kind, cz_group, inter, right, acc)


def local(intersections, screened, poles, gap_energy, gap_class):
    zl, c = lax.axis_index("zl"), lax.axis_index("c")
    column = lax.axis_index("zh") * lax.axis_size("x") + lax.axis_index("x")
    place = jnp.stack([zl, c, column]).astype(jnp.int32)
    swap = [(0, 1), (1, 0)]
    per = lax.axis_size("y")
    own, square, kind = prepare(screened, poles, gap_energy, gap_class, per)
    y_group = lax.all_to_all(own, "y", 0, 0, tiled=True)
    z_group = lax.ppermute(y_group, "zl", swap)
    cy_group = lax.ppermute(y_group, "c", swap)
    acc, same, cross, right = first(place, square, y_group, cy_group, intersections)
    cz_group = lax.ppermute(z_group, "c", swap)
    acc = second(square, z_group, same, acc)
    full = third(square, kind, cz_group, cross, right, acc)
    pair = lax.all_to_all(full, "c", 0, 0, tiled=True)
    chip = pair[0] + pair[1]
    pieces = lax.all_to_all(chip.astype(BF16), ("zl", "y"), 0, 0, tiled=True)
    rows = jnp.sum(pieces.astype(F32), axis=0)
    high, low = lax.axis_size("zh"), lax.axis_size("x")
    fine = rows.shape[0]
    split = rows.reshape(fine, high, low, -1).transpose(2, 1, 0, 3)
    wide = split.shape[3]
    blocks = lax.all_to_all(split.reshape(high * low, fine * wide), ("x", "zh"), 0, 0, tiled=True)
    total = jnp.sum(blocks, axis=0).reshape(fine, wide)
    count = intersections.shape[1] * intersections.shape[0] * 2 * per * 2
    return total * (1.0 / jnp.sqrt(F32(count)))


def solution(mesh):
    fine = Mesh(mesh.devices.reshape(2, 8, 2, 4, 8), ("zl", "y", "c", "zh", "x"))
    band, col = ("zl", "y", "c"), ("zh", "x")
    return jax.shard_map(
        local,
        mesh=fine,
        in_specs=(P(band, None, None), P(band, col), P(band, col), P(), P(band, None)),
        out_specs=P(band, col),
        check_vma=False,
    )
```
